32 devices in a mesh: wide: 16 (over z, y, x), band: 2 (over core).
Axes of the slice: x: 2, y: 2, z: 4, core: 2. Of those that a mesh axis runs over, the one named last changes fastest.
Arguments:
- prior_states: bfloat16 [256, 2, 64, 8, 128], P('wide', 'band'), may hold values from -6 to 6
- measured_anomalies: bfloat16 [2, 64, 256, 128], P('band', 'wide'), may hold values from -6 to 6
- departures: bfloat16 [2, 64, 128], P('band', 'wide'), may hold values from -15 to 15
- error_precisions: bfloat16 [2, 64, 128], P('band', 'wide'), may hold values from 0.25 to 4
- datum_totals: int32 [2, 64], P('band', 'wide'), may hold values from 64 to 128, as said below
- datum_patch_owner: int32 [2, 64, 128], P('band', 'wide'), may hold values from 0 to 3
- patch_group_lookup: int32 [2, 64, 4], P('band', 'wide'), may hold values from 0 to 11, as said below
Outputs:
- analysis: bfloat16 [256, 2, 64, 8, 128], P('wide', 'band')
The draws below stay inside these ranges and needn't reach their ends.
Inputs may be any that keep to these rules, and one draw needn't show every extreme that they name: The observations of a block fill its first datum_totals slots; in every band some block is full (128). `patch_group_lookup`: entry 0 of every list lies below 4 (a block of the band below), entry 1 at 8 or above (a block of the band above), and the other entries are distinct blocks of the tile's own band, from 4 to 7.
All inputs are finite; a program needn't handle non-finite values.
Results may differ from the reference program's by a relative error of at most 0.0062.
Values may be sent and summed in bfloat16 or wider, within the bound.
No kernel may reach another device: no remote copies, remote signals or barrier semaphores. Data moves between devices by JAX's collectives and lax.ppermute only.
A program may use at most 64 MiB of HBM per device.

```python
import math
import jax
import jax.numpy as jnp
from jax import lax

SAMPLE_TOTAL = 256
LAYER_DEPTH = 8
PATCH_VERTICALS = 128
TILES_DEV = 4
BSIZE = 128
BLK_DEV = 4
NLIST = 4
NS_ITERS = 6
ZONAL_BELTS = 2
ZONE_PATCHES = 64
BLOCKS = 64


def draw_datum_totals(key, part):
    first, second, third = jax.random.split(key, 3)
    left = jax.random.randint(first, (ZONAL_BELTS, BLOCKS), 0, BSIZE)
    right = jax.random.randint(second, (ZONAL_BELTS, BLOCKS), 0, BSIZE)
    counts = BSIZE // 2 + left * right // (2 * BSIZE)
    full_at = jax.random.randint(third, (ZONAL_BELTS, 1), 0, BLOCKS)
    half_at = (full_at + 1) % BLOCKS
    position = jnp.arange(BLOCKS, dtype=jnp.int32)[None, :]
    counts = jnp.where(position == half_at, BSIZE // 2, counts)
    return jnp.where(position == full_at, BSIZE, counts).astype(jnp.int32)


def draw_patch_group_lookup(key, part):
    first, second, third = jax.random.split(key, 3)
    below = jax.random.randint(first, (ZONAL_BELTS, ZONE_PATCHES, 1), 0, BLK_DEV)
    above = jax.random.randint(second, (ZONAL_BELTS, ZONE_PATCHES, 1), 2 * BLK_DEV, 3 * BLK_DEV)
    several = jax.random.split(third, ZONAL_BELTS * ZONE_PATCHES)
    order = jax.vmap(lambda single: jax.random.permutation(single, BLK_DEV))(several)
    own = order[:, :NLIST - 2].reshape(ZONAL_BELTS, ZONE_PATCHES, NLIST - 2) + BLK_DEV
    return jnp.concatenate([below.astype(jnp.int32), above.astype(jnp.int32), own.astype(jnp.int32)], axis=2)


def touch_ends(array, own_key, smallest, high):
    spot = [jax.random.randint(jax.random.fold_in(own_key, axis), (), 0, length) for axis, length in enumerate(array.shape)]
    widest = array.shape.index(max(array.shape))
    neighbour = spot[:widest] + [(spot[widest] + 1) % array.shape[widest]] + spot[widest + 1:]
    return array.at[tuple(spot)].set(smallest).at[tuple(neighbour)].set(high)


def level_of(key, dims, shards, least, top_value):
    def one(dim, parts):
        heights = jax.random.uniform(jax.random.fold_in(jax.random.fold_in(key, 6), dim), (parts,), jnp.float32, least / len(shards), top_value / len(shards))
        return jnp.repeat(jnp.exp(heights), dims[dim] // parts).reshape((-1,) + (1,) * (len(dims) - dim - 1))

    gain = one(*shards[0])
    for cut in shards[1:]:
        gain = gain * one(*cut)
    return gain


def bell_draw(own_key, extent, width, limit, pieces=(), kind=jnp.bfloat16):
    drawn = jax.random.normal(own_key, extent, jnp.float32) * width
    if len(pieces) > 0:
        drawn = level_of(own_key, extent, pieces, -0.22, 0.18) * drawn
    return jnp.clip(drawn, min=-limit, max=limit).astype(kind)


def setup_inputs(seed: int = 0) -> dict:
    streams_of = jax.random.split(jax.random.key(seed), 8)
    return {
        "prior_states": bell_draw(streams_of[0], (SAMPLE_TOTAL, ZONAL_BELTS, ZONE_PATCHES, LAYER_DEPTH, PATCH_VERTICALS), 1.0, 6.0, ((0, 16), (1, 2))),
        "measured_anomalies": bell_draw(streams_of[1], (ZONAL_BELTS, BLOCKS, SAMPLE_TOTAL, BSIZE), 1.0, 6.0, ((0, 2), (1, 16))),
        "departures": bell_draw(streams_of[2], (ZONAL_BELTS, BLOCKS, BSIZE), 3.0, 15.0, ((0, 2), (1, 16))),
        "error_precisions": jnp.clip(jnp.exp(math.log(4.0) - 2.7725887 * jax.random.uniform(streams_of[3], (ZONAL_BELTS, BLOCKS, BSIZE), jnp.float32) ** level_of(streams_of[3], (ZONAL_BELTS, BLOCKS, BSIZE), ((0, 2), (1, 16)), -0.2, 0.2)), 0.25, 4.0).astype(jnp.bfloat16),
        "datum_totals": draw_datum_totals(jax.random.fold_in(streams_of[7], 71), 0),
        "datum_patch_owner": touch_ends(jax.random.randint(streams_of[5], (ZONAL_BELTS, BLOCKS, BSIZE), 0, TILES_DEV), jax.random.fold_in(streams_of[5], 1), 0, TILES_DEV - 1).astype(jnp.int32),
        "patch_group_lookup": draw_patch_group_lookup(jax.random.fold_in(streams_of[7], 71), 0),
    }


LOC_FAR = 0.5
HIGH = lax.Precision.HIGHEST

def newton_roots(precision_matrix, identity):
    norm_c = jnp.sqrt(jnp.sum(precision_matrix * precision_matrix))
    current = precision_matrix / norm_c
    root_inv = identity
    for sweep in range(NS_ITERS):
        factor = 1.5 * identity - 0.5 * jnp.dot(root_inv, current, precision=HIGH)
        current = jnp.dot(current, factor, precision=HIGH)
        root_inv = jnp.dot(factor, root_inv, precision=HIGH)
    return (root_inv, norm_c)

def reference(prior_states, measured_anomalies, departures, error_precisions, datum_totals, datum_patch_owner, patch_group_lookup):
    sample_states = prior_states.shape[0]
    identity = jnp.eye(sample_states, dtype=jnp.float32)
    padded_pert = jnp.pad(measured_anomalies, ((1, 1), (0, 0), (0, 0), (0, 0)))
    padded_innov = jnp.pad(departures, ((1, 1), (0, 0), (0, 0)))
    padded_var = jnp.pad(error_precisions, ((1, 1), (0, 0), (0, 0)))
    padded_count = jnp.pad(datum_totals, ((1, 1), (0, 0)))
    padded_home = jnp.pad(datum_patch_owner, ((1, 1), (0, 0), (0, 0)))
    slot_index = jnp.arange(BSIZE, dtype=jnp.int32)

    def one_tile(pair):
        zonal_belt = (pair // ZONE_PATCHES).astype(jnp.int32)
        mesh_patch = (pair % ZONE_PATCHES).astype(jnp.int32)
        column = mesh_patch // TILES_DEV
        local = mesh_patch % TILES_DEV
        names = patch_group_lookup[zonal_belt, mesh_patch]
        source_band = (zonal_belt + names // BLK_DEV).astype(jnp.int32)
        source_block = (column * BLK_DEV + names % BLK_DEV).astype(jnp.int32)
        pert = padded_pert[source_band, source_block]
        innov = padded_innov[source_band, source_block]
        live = slot_index[None, :] < padded_count[source_band, source_block][:, None]
        near = padded_home[source_band, source_block] == local
        weights = padded_var[source_band, source_block].astype(jnp.float32)
        weights = weights * jnp.where(live, 1.0, 0.0) * jnp.where(near, 1.0, LOC_FAR)
        pert_mat = jnp.transpose(pert, (1, 0, 2)).reshape(sample_states, NLIST * BSIZE)
        scaled = (pert_mat.astype(jnp.float32) * weights.reshape(-1)).astype(jnp.bfloat16)
        precision_matrix = (sample_states - 1) * identity + jnp.dot(scaled, pert_mat.T, preferred_element_type=jnp.float32)
        drive = jnp.dot(scaled, innov.reshape(-1), preferred_element_type=jnp.float32)
        root_inv, norm_c = newton_roots(precision_matrix, identity)
        inner = jnp.dot(root_inv, drive, precision=HIGH)
        gain_vec = jnp.dot(root_inv, inner, precision=HIGH) / norm_c
        mix = (jnp.sqrt((sample_states - 1) / norm_c) * root_inv + gain_vec[:, None]).astype(jnp.bfloat16)
        state_quantities = prior_states[:, zonal_belt, mesh_patch].reshape(sample_states, LAYER_DEPTH * PATCH_VERTICALS)
        mean_field = lax.optimization_barrier(jnp.sum(state_quantities.astype(jnp.float32), axis=0)) / sample_states
        spread = (state_quantities.astype(jnp.float32) - mean_field).astype(jnp.bfloat16)
        result = mean_field + jnp.dot(mix.T, spread, preferred_element_type=jnp.float32)
        return result.astype(jnp.bfloat16).reshape(sample_states, LAYER_DEPTH, PATCH_VERTICALS)
    pairs = jnp.arange(ZONAL_BELTS * ZONE_PATCHES, dtype=jnp.int32)
    result = lax.map(one_tile, pairs)
    result = result.reshape(ZONAL_BELTS, ZONE_PATCHES, sample_states, LAYER_DEPTH, PATCH_VERTICALS)
    return jnp.transpose(result, (2, 0, 1, 3, 4))
```

```python
import functools

import jax
import jax.numpy as jnp
from jax import lax
from jax.experimental import pallas as pl
from jax.experimental.pallas import tpu as pltpu
from jax.sharding import PartitionSpec as P


NS_ITERS = 6
LOC_FAR = 0.5
DIRECT_MAX = 16


def split(x):
    high = x.astype(jnp.bfloat16)
    return high, (x - high.astype(jnp.float32)).astype(jnp.bfloat16)


def dot3(a, b):
    (ah, al), (bh, bl) = a, b
    dot = functools.partial(jnp.dot, preferred_element_type=jnp.float32)
    return dot(ah, bh) + (dot(ah, bl) + dot(al, bh))


def mix_kernel(groups, lists, spot, own, below, above, own_aux, below_aux, above_aux, mix, pert_buf):
    tiles, members, _ = mix.shape
    slots = own.shape[2]
    entries = lists.shape[1]
    blocks = own.shape[0]
    rows = members // groups
    me = spot[0]
    contract_last = (((1,), (1,)), ((), ()))
    row = lax.broadcasted_iota(jnp.int32, (members, members), 0)
    col = lax.broadcasted_iota(jnp.int32, (members, members), 1)
    eye = jnp.where(row == col, 1.0, 0.0).astype(jnp.float32)
    state = []
    for t in range(tiles):
        weights, innovs = [], []
        for n in range(entries):
            name = lists[t, n]
            if n == 0:
                src, aux, block = below, below_aux, name
            elif n == 1:
                src, aux, block = above, above_aux, name - 2 * blocks
            else:
                src, aux, block = own, own_aux, name - blocks
            for u in range(groups):
                start = 0 if groups == 1 else pl.multiple_of((me ^ u) * rows, rows)
                pert_buf[t, u * rows:(u + 1) * rows, n * slots:(n + 1) * slots] = src[
                    block, pl.ds(start, rows), :
                ]
            weights.append(aux[block, t:t + 1, :])
            innovs.append(aux[block, tiles:tiles + 1, :])
        pert = pert_buf[t]
        weight = jnp.concatenate(weights, axis=1)
        innov = jnp.concatenate(innovs, axis=1)
        scaled = (pert.astype(jnp.float32) * weight).astype(jnp.bfloat16)
        precision = (members - 1) * eye + lax.dot_general(
            pert, scaled, contract_last, preferred_element_type=jnp.float32
        )
        drive = lax.dot_general(
            jnp.broadcast_to(innov, (8, innov.shape[1])).astype(jnp.bfloat16),
            scaled,
            contract_last,
            preferred_element_type=jnp.float32,
        )
        square = jnp.sum(precision * precision, axis=0, keepdims=True)
        norm = jnp.sqrt(jnp.sum(square, axis=1, keepdims=True))
        state.append((precision / norm, drive, norm))
    currents = [s[0] for s in state]
    roots = [None] * tiles
    for sweep in range(NS_ITERS):
        for t in range(tiles):
            current = split(currents[t])
            if sweep == 0:
                factor = 1.5 * eye - 0.5 * currents[t]
            else:
                factor = 1.5 * eye - 0.5 * dot3(current, split(roots[t]))
            both = split(factor)
            if sweep < NS_ITERS - 1:
                currents[t] = dot3(both, current)
            roots[t] = factor if sweep == 0 else dot3(split(roots[t]), both)
    for t in range(tiles):
        _, drive, norm = state[t]
        root = split(roots[t])
        inner = dot3(split(drive), root)
        gain = dot3(split(inner), root) / norm
        scale = jnp.sqrt((members - 1) / norm)
        mix[t] = (scale * roots[t] + gain[0:1, :]).astype(jnp.bfloat16)


def analysis_kernel(pieces, mix, *refs):
    arrived, sent = refs[:pieces], refs[pieces:2 * pieces]
    spread_buf, out_buf = refs[2 * pieces:]
    tiles, members, _ = mix.shape
    rows = members // pieces
    depth, points = arrived[0].shape[2:]
    for t in range(tiles):
        mean = jnp.zeros((depth, points), jnp.float32)
        for u in range(pieces):
            mean += jnp.sum(arrived[u][:, t].astype(jnp.float32), axis=0)
        mean = mean / members
        for u in range(pieces):
            spread = arrived[u][:, t].astype(jnp.float32) - mean
            spread_buf[u * rows * depth:(u + 1) * rows * depth, :] = spread.reshape(
                rows * depth, points
            )
        step = 2 if depth % 2 == 0 else 1
        for level in range(0, depth, step):
            field = jnp.concatenate(
                [
                    spread_buf[pl.ds(level + k, members, stride=depth), :].astype(jnp.bfloat16)
                    for k in range(step)
                ],
                axis=1,
            )
            result = jnp.dot(mix[t], field, preferred_element_type=jnp.float32)
            for k in range(step):
                out_buf[pl.ds(level + k, members, stride=depth), :] = (
                    result[:, k * points:(k + 1) * points] + mean[level + k:level + k + 1, :]
                )
        for u in range(pieces):
            sent[u][:, t] = (
                out_buf[u * rows * depth:(u + 1) * rows * depth, :]
                .reshape(rows, depth, points)
                .astype(jnp.bfloat16)
            )


def neighbours(x, axis):
    peers = lax.axis_size(axis)
    if peers == 1:
        return x, x
    if peers == 2:
        other = lax.ppermute(x, axis, [(0, 1), (1, 0)])
        return other, other
    up = [(i, i + 1) for i in range(peers - 1)]
    return lax.ppermute(x, axis, up), lax.ppermute(x, axis, [(j, i) for i, j in up])


def send_order(wide):
    far = list(range(wide // 2, wide))
    half = len(far) // 2
    mixed = [s for pair in zip(far[half:], far[:half]) for s in pair]
    return mixed + list(range(1, wide // 2))


def on_device(
    prior_states,
    measured_anomalies,
    departures,
    error_precisions,
    datum_totals,
    datum_patch_owner,
    patch_group_lookup,
):
    wide = lax.axis_size("wide")
    bands = lax.axis_size("band")
    me = lax.axis_index("wide").astype(jnp.int32)
    direct = wide <= DIRECT_MAX
    mine, _, _, depth, points = prior_states.shape
    blocks, members, slots = measured_anomalies.shape[1:]
    tiles = patch_group_lookup.shape[1]
    fields = prior_states.reshape(mine, wide, tiles, depth, points)

    if direct:
        arrived = {0: lax.dynamic_index_in_dim(fields, me, 1, keepdims=False)}
        for s in send_order(wide):
            part = lax.dynamic_index_in_dim(fields, me ^ s, 1, keepdims=False)
            arrived[s] = lax.ppermute(part, "wide", [(i, i ^ s) for i in range(wide)])
        arrived = [arrived[s] for s in range(wide)]
    else:
        arrived = [
            lax.all_to_all(fields, "wide", split_axis=1, concat_axis=0, tiled=True).reshape(
                members, tiles, depth, points
            )
        ]
    pieces = len(arrived)

    slot_index = jnp.arange(slots, dtype=jnp.int32)
    live = jnp.where(slot_index[None, :] < datum_totals[0][:, None], 1.0, 0.0)
    base = error_precisions[0].astype(jnp.float32) * live
    tile_ids = jnp.arange(tiles, dtype=jnp.int32)
    near = jnp.where(datum_patch_owner[0][:, None, :] == tile_ids[None, :, None], 1.0, LOC_FAR)
    pad = -(tiles + 1) % 8
    aux = jnp.concatenate(
        [
            base[:, None, :] * near,
            departures[0][:, None, :].astype(jnp.float32),
            jnp.zeros((blocks, pad, slots), jnp.float32),
        ],
        axis=1,
    )
    below, above = neighbours(measured_anomalies[0], "band")
    below_aux, above_aux = neighbours(aux, "band")
    band = lax.axis_index("band")
    below_aux = jnp.where(band > 0, below_aux, 0.0)
    above_aux = jnp.where(band < bands - 1, above_aux, 0.0)

    vmem = pl.BlockSpec(memory_space=pltpu.VMEM)
    smem = pl.BlockSpec(memory_space=pltpu.SMEM)
    mix = pl.pallas_call(
        functools.partial(mix_kernel, pieces),
        out_shape=jax.ShapeDtypeStruct((tiles, members, members), jnp.bfloat16),
        in_specs=[smem, smem] + [vmem] * 6,
        out_specs=vmem,
        scratch_shapes=[
            pltpu.VMEM((tiles, members, patch_group_lookup.shape[2] * slots), jnp.bfloat16)
        ],
        name="mix",
    )(
        patch_group_lookup[0],
        me.reshape(1),
        measured_anomalies[0],
        below,
        above,
        aux,
        below_aux,
        above_aux,
    )
    rows = members // pieces
    sent = pl.pallas_call(
        functools.partial(analysis_kernel, pieces),
        out_shape=[jax.ShapeDtypeStruct((rows, tiles, depth, points), jnp.bfloat16)] * pieces,
        in_specs=[vmem] * (1 + pieces),
        out_specs=[vmem] * pieces,
        scratch_shapes=[pltpu.VMEM((members * depth, points), jnp.float32)] * 2,
        name="analysis",
    )(mix, *arrived)

    if not direct:
        back = lax.all_to_all(
            sent[0].reshape(wide, mine, tiles, depth, points),
            "wide",
            split_axis=0,
            concat_axis=2,
            tiled=True,
        )
        return back.reshape(prior_states.shape)
    result = jnp.zeros(fields.shape, jnp.bfloat16)
    result = lax.dynamic_update_index_in_dim(result, sent[0], me, 1)
    back = {}
    for s in send_order(wide):
        back[s] = lax.ppermute(sent[s], "wide", [(i, i ^ s) for i in range(wide)])
    for s in send_order(wide):
        result = lax.dynamic_update_index_in_dim(result, back[s], me ^ s, 1)
    return result.reshape(prior_states.shape)


def solution(mesh):
    in_specs = (
        P("wide", "band", None, None, None),
        P("band", "wide", None, None),
        P("band", "wide", None),
        P("band", "wide", None),
        P("band", "wide"),
        P("band", "wide", None),
        P("band", "wide", None),
    )
    out_specs = P("wide", "band", None, None, None)
    return jax.shard_map(
        on_device, mesh=mesh, in_specs=in_specs, out_specs=out_specs, check_vma=False
    )
```

```python
import functools

import jax
import jax.numpy as jnp
from jax import lax
from jax.experimental import pallas as pl
from jax.experimental.pallas import tpu as pltpu
from jax.sharding import PartitionSpec as P


NS_ITERS = 6
LOC_FAR = 0.5
DIRECT_MAX = 16

LATE = 2
MIB = 1 << 20


def split(x):
    high = x.astype(jnp.bfloat16)
    return high, (x - high.astype(jnp.float32)).astype(jnp.bfloat16)


def dot3(a, b):
    (ah, al), (bh, bl) = a, b
    dot = functools.partial(jnp.dot, preferred_element_type=jnp.float32)
    return dot(ah, bh) + (dot(ah, bl) + dot(al, bh))


def mix_kernel(order, lists, spot, own, below, above, own_aux, below_aux, above_aux, mix, rest, pert_buf):
    tiles, members, _ = mix.shape
    slots = own.shape[2]
    entries = lists.shape[1]
    blocks = own.shape[0]
    rows = members // len(order)
    me = spot[0]
    contract_last = (((1,), (1,)), ((), ()))
    row = lax.broadcasted_iota(jnp.int32, (members, members), 0)
    col = lax.broadcasted_iota(jnp.int32, (members, members), 1)
    eye = jnp.where(row == col, 1.0, 0.0).astype(jnp.float32)
    state = []
    for t in range(tiles):
        weights, innovs = [], []
        for n in range(entries):
            name = lists[t, n]
            if n == 0:
                src, aux, block = below, below_aux, name
            elif n == 1:
                src, aux, block = above, above_aux, name - 2 * blocks
            else:
                src, aux, block = own, own_aux, name - blocks
            for q, u in enumerate(order):
                start = 0 if len(order) == 1 else pl.multiple_of((me ^ u) * rows, rows)
                pert_buf[t, q * rows:(q + 1) * rows, n * slots:(n + 1) * slots] = src[
                    block, pl.ds(start, rows), :
                ]
            weights.append(aux[block, t:t + 1, :])
            innovs.append(aux[block, tiles:tiles + 1, :])
        pert = pert_buf[t]
        weight = jnp.concatenate(weights, axis=1)
        innov = jnp.concatenate(innovs, axis=1)
        scaled = (pert.astype(jnp.float32) * weight).astype(jnp.bfloat16)
        precision = (members - 1) * eye + lax.dot_general(
            pert, scaled, contract_last, preferred_element_type=jnp.float32
        )
        drive = lax.dot_general(
            jnp.broadcast_to(innov, (8, innov.shape[1])).astype(jnp.bfloat16),
            scaled,
            contract_last,
            preferred_element_type=jnp.float32,
        )
        square = jnp.sum(precision * precision, axis=0, keepdims=True)
        norm = jnp.sqrt(jnp.sum(square, axis=1, keepdims=True))
        state.append((precision / norm, drive, norm))
    currents = [s[0] for s in state]
    roots = [None] * tiles
    for sweep in range(NS_ITERS):
        for t in range(tiles):
            current = split(currents[t])
            if sweep == 0:
                factor = 1.5 * eye - 0.5 * currents[t]
            else:
                factor = 1.5 * eye - 0.5 * dot3(current, split(roots[t]))
            both = split(factor)
            if sweep < NS_ITERS - 1:
                currents[t] = dot3(both, current)
            roots[t] = factor if sweep == 0 else dot3(split(roots[t]), both)
    for t in range(tiles):
        _, drive, norm = state[t]
        root = split(roots[t])
        inner = dot3(split(drive), root)
        gain = dot3(split(inner), root) / norm
        scale = jnp.sqrt((members - 1) / norm)
        final = (scale * roots[t] + gain[0:1, :]).astype(jnp.bfloat16)
        mix[t] = final
        left = 1.0 - jnp.sum(final.astype(jnp.float32), axis=1, keepdims=True)
        rest[t] = jnp.broadcast_to(left, rest.shape[1:])


def turn_in(piece, t, buf):
    rows, _, depth, points = piece.shape
    field = piece[:, t].astype(jnp.float32)
    buf[...] = field.reshape(rows * depth, points)
    turned = jnp.concatenate(
        [buf[pl.ds(level, rows, stride=depth), :] for level in range(depth)], axis=1
    )
    return turned.astype(jnp.bfloat16), jnp.sum(field, axis=0)


def gather_kernel(*refs):
    pieces, (fields, total, bufs) = refs[:-3], refs[-3:]
    rows = pieces[0].shape[0]
    for t in range(fields.shape[0]):
        acc = jnp.zeros(total.shape[1:], jnp.float32)
        for q, piece in enumerate(pieces):
            turned, part = turn_in(piece, t, bufs.at[(t * len(pieces) + q) % bufs.shape[0]])
            fields[t, q * rows:(q + 1) * rows, :] = turned
            acc += part
        total[t] = acc


def combine(t, mix, rest, field, mean, sent, first):
    _, depth, rows, points = sent[0].shape
    count = len(sent) * rows
    result = jnp.dot(
        mix[t, first:first + count, :], field, preferred_element_type=jnp.float32
    )
    for level in range(depth):
        part = result[:, level * points:(level + 1) * points]
        part = part + rest[t, first:first + count, :] * mean[level:level + 1, :]
        part = part.astype(jnp.bfloat16)
        for v, out in enumerate(sent):
            out[t, level] = part[v * rows:(v + 1) * rows, :]


def first_kernel(late, first, mix, rest, fields, total, *refs):
    pieces, sent = refs[:late], refs[late:-3]
    late_fields, mean_out, bufs = refs[-3:]
    tiles, members, _ = mix.shape
    rows = pieces[0].shape[0]
    for t in range(tiles):
        acc = total[t]
        turned = [fields[t]]
        for q, piece in enumerate(pieces):
            part, add = turn_in(piece, t, bufs.at[t * late + q])
            late_fields[t, q * rows:(q + 1) * rows, :] = part
            turned.append(part)
            acc += add
        mean = acc / members
        mean_out[t] = mean
        combine(t, mix, rest, jnp.concatenate(turned, axis=0), mean, sent, first)


def second_kernel(mix, rest, fields, late_fields, mean, *sent):
    for t in range(mix.shape[0]):
        field = jnp.concatenate([fields[t], late_fields[t]], axis=0)
        combine(t, mix, rest, field, mean[t], sent, 0)


def place_kernel(order, aliased, spot, *refs):
    pieces = refs[:len(order)]
    result, turned, buf, sems = refs[len(order) + aliased:]
    tiles, depth, rows, points = pieces[0].shape
    copies = []
    for q, (u, piece) in enumerate(zip(order, pieces)):
        for t in range(tiles):
            view = buf.at[(q * tiles + t) % buf.shape[0]]
            for level in range(depth):
                view[pl.ds(level, rows, stride=depth), :] = piece[t, level].astype(jnp.float32)
            turned[q, :, t] = view[...].reshape(rows, depth, points).astype(jnp.bfloat16)
        copy = pltpu.make_async_copy(turned.at[q], result.at[:, spot[0] ^ u], sems.at[q])
        copy.start()
        copies.append(copy)
    for copy in copies:
        copy.wait()


def neighbours(x, axis):
    peers = lax.axis_size(axis)
    if peers == 1:
        return x, x
    if peers == 2:
        other = lax.ppermute(x, axis, [(0, 1), (1, 0)])
        return other, other
    up = [(i, i + 1) for i in range(peers - 1)]
    return lax.ppermute(x, axis, up), lax.ppermute(x, axis, [(j, i) for i, j in up])


def send_order(wide):
    far = list(range(wide // 2, wide))
    half = len(far) // 2
    return [s for pair in zip(far[half:], far[:half]) for s in pair], list(range(1, wide // 2))


def on_device(
    prior_states,
    measured_anomalies,
    departures,
    error_precisions,
    datum_totals,
    datum_patch_owner,
    patch_group_lookup,
):
    wide = lax.axis_size("wide")
    bands = lax.axis_size("band")
    me = lax.axis_index("wide").astype(jnp.int32)
    direct = wide <= DIRECT_MAX
    mine, _, _, depth, points = prior_states.shape
    blocks, members, slots = measured_anomalies.shape[1:]
    tiles, entries = patch_group_lookup.shape[1:]
    fields = prior_states.reshape(mine, wide, tiles, depth, points)
    vmem = pl.BlockSpec(memory_space=pltpu.VMEM)
    smem = pl.BlockSpec(memory_space=pltpu.SMEM)

    def call(kernel, out_shape, in_specs, scratch, limit, **more):
        out_specs = more.pop("out_specs", jax.tree.map(lambda _: vmem, out_shape))
        return pl.pallas_call(
            kernel,
            out_shape=out_shape,
            in_specs=in_specs,
            out_specs=out_specs,
            scratch_shapes=scratch,
            compiler_params=pltpu.CompilerParams(vmem_limit_bytes=limit * MIB),
            **more,
        )

    def swap(x, s):
        return lax.ppermute(x, "wide", [(i, i ^ s) for i in range(wide)])

    if direct:
        far, near_by = send_order(wide)
        arrived = {}
        left = fields
        for group in (far[:2], far[2:], near_by + [0]):
            parts = [lax.dynamic_index_in_dim(left, me ^ s, 1, keepdims=False) for s in group]
            left, *parts = lax.optimization_barrier((left, *parts))
            for s, part in zip(group, parts):
                if s == 0:
                    arrived[0] = part
                    continue
                arrived[s] = swap(part, s)
        late = far[-1:-2 * LATE:-2]
        early = [0] + near_by + [s for s in far if s not in late]
        order = early + late
    else:
        order = [0]

    slot_index = jnp.arange(slots, dtype=jnp.int32)
    live = jnp.where(slot_index[None, :] < datum_totals[0][:, None], 1.0, 0.0)
    base = error_precisions[0].astype(jnp.float32) * live
    tile_ids = jnp.arange(tiles, dtype=jnp.int32)
    near = jnp.where(datum_patch_owner[0][:, None, :] == tile_ids[None, :, None], 1.0, LOC_FAR)
    pad = -(tiles + 1) % 8
    aux = jnp.concatenate(
        [
            base[:, None, :] * near,
            departures[0][:, None, :].astype(jnp.float32),
            jnp.zeros((blocks, pad, slots), jnp.float32),
        ],
        axis=1,
    )
    below, above = neighbours(measured_anomalies[0], "band")
    below_aux, above_aux = neighbours(aux, "band")
    band = lax.axis_index("band")
    below_aux = jnp.where(band > 0, below_aux, 0.0)
    above_aux = jnp.where(band < bands - 1, above_aux, 0.0)

    mix, rest = call(
        functools.partial(mix_kernel, order),
        [
            jax.ShapeDtypeStruct((tiles, members, members), jnp.bfloat16),
            jax.ShapeDtypeStruct((tiles, members, points), jnp.float32),
        ],
        [smem, smem] + [vmem] * 6,
        [pltpu.VMEM((tiles, members, entries * slots), jnp.bfloat16)],
        24,
    )(
        patch_group_lookup[0],
        me.reshape(1),
        measured_anomalies[0],
        below,
        above,
        aux,
        below_aux,
        above_aux,
    )

    if not direct:
        whole = lax.all_to_all(fields, "wide", split_axis=1, concat_axis=0, tiled=True)
        flat = whole.reshape(members, tiles, depth * points)
        mean = jnp.sum(flat, axis=0, dtype=jnp.float32) / members
        spread = (flat.astype(jnp.float32) - mean).astype(jnp.bfloat16)
        result = mean + jnp.einsum("tkj,jtp->ktp", mix, spread, preferred_element_type=jnp.float32)
        back = lax.all_to_all(
            result.astype(jnp.bfloat16).reshape(wide, mine, tiles, depth, points),
            "wide",
            split_axis=0,
            concat_axis=2,
            tiled=True,
        )
        return back.reshape(prior_states.shape)

    width = depth * points
    count = len(early) * mine
    gathered, total = call(
        gather_kernel,
        [
            jax.ShapeDtypeStruct((tiles, count, width), jnp.bfloat16),
            jax.ShapeDtypeStruct((tiles, depth, points), jnp.float32),
        ],
        [vmem] * len(early),
        [pltpu.VMEM((8, mine * depth, points), jnp.float32)],
        12,
    )(*[arrived[s] for s in early])
    piece = jax.ShapeDtypeStruct((tiles, depth, mine, points), jnp.bfloat16)
    close = len(near_by) + 1
    *sent_far, late_fields, mean = call(
        functools.partial(first_kernel, len(late), close * mine),
        [piece] * (len(order) - close)
        + [
            jax.ShapeDtypeStruct((tiles, len(late) * mine, width), jnp.bfloat16),
            jax.ShapeDtypeStruct((tiles, depth, points), jnp.float32),
        ],
        [vmem] * (4 + len(late)),
        [pltpu.VMEM((tiles * len(late), mine * depth, points), jnp.float32)],
        12,
    )(mix, rest, gathered, total, *[arrived[s] for s in late])
    sent_near = call(
        second_kernel, [piece] * close, [vmem] * 5, [], 12
    )(mix, rest, gathered, late_fields, mean)
    sent = dict(zip(order, list(sent_near) + sent_far))
    back = {0: sent[0]}
    for s in far + near_by:
        back[s] = swap(sent[s], s)

    result = jax.ShapeDtypeStruct((mine, wide, tiles, depth, points), jnp.bfloat16)
    hbm = pl.BlockSpec(memory_space=pl.ANY)

    def place(group, *rest):
        return call(
            functools.partial(place_kernel, group, len(rest)),
            result,
            [smem] + [vmem] * len(group) + [hbm] * len(rest),
            [
                pltpu.VMEM((len(group), mine, tiles, depth, points), jnp.bfloat16),
                pltpu.VMEM((4, mine * depth, points), jnp.float32),
                pltpu.SemaphoreType.DMA((len(group),)),
            ],
            12,
            out_specs=hbm,
            input_output_aliases={1 + len(group): 0} if rest else {},
        )(me.reshape(1), *[back[s] for s in group], *rest)

    most = place(early)
    return place(late, most).reshape(prior_states.shape)


def solution(mesh):
    in_specs = (
        P("wide", "band", None, None, None),
        P("band", "wide", None, None),
        P("band", "wide", None),
        P("band", "wide", None),
        P("band", "wide"),
        P("band", "wide", None),
        P("band", "wide", None),
    )
    out_specs = P("wide", "band", None, None, None)
    return jax.shard_map(
        on_device, mesh=mesh, in_specs=in_specs, out_specs=out_specs, check_vma=False
    )
```

```python
import functools

import jax
import jax.numpy as jnp
from jax import lax
from jax.experimental import pallas as pl
from jax.experimental.pallas import tpu as pltpu
from jax.sharding import PartitionSpec as P


NS_ITERS = 6
LOC_FAR = 0.5
DIRECT_MAX = 16

LATE = 4
LEAD = 2
MIB = 1 << 20


def split(x):
    high = x.astype(jnp.bfloat16)
    return high, (x - high.astype(jnp.float32)).astype(jnp.bfloat16)


def dot3(a, b):
    (ah, al), (bh, bl) = a, b
    dot = functools.partial(jnp.dot, preferred_element_type=jnp.float32)
    return dot(ah, bh) + (dot(ah, bl) + dot(al, bh))


def mix_kernel(order, lists, spot, own, below, above, own_aux, below_aux, above_aux, mix, rest, pert_buf):
    tiles, members, _ = mix.shape
    slots = own.shape[2]
    entries = lists.shape[1]
    blocks = own.shape[0]
    rows = members // len(order)
    me = spot[0]
    contract_last = (((1,), (1,)), ((), ()))
    row = lax.broadcasted_iota(jnp.int32, (members, members), 0)
    col = lax.broadcasted_iota(jnp.int32, (members, members), 1)
    eye = jnp.where(row == col, 1.0, 0.0).astype(jnp.float32)
    state = []
    for t in range(tiles):
        weights, innovs = [], []
        for n in range(entries):
            name = lists[t, n]
            if n == 0:
                src, aux, block = below, below_aux, name
            elif n == 1:
                src, aux, block = above, above_aux, name - 2 * blocks
            else:
                src, aux, block = own, own_aux, name - blocks
            for q, u in enumerate(order):
                start = 0 if len(order) == 1 else pl.multiple_of((me ^ u) * rows, rows)
                pert_buf[t, q * rows:(q + 1) * rows, n * slots:(n + 1) * slots] = src[
                    block, pl.ds(start, rows), :
                ]
            weights.append(aux[block, t:t + 1, :])
            innovs.append(aux[block, tiles:tiles + 1, :])
        pert = pert_buf[t]
        weight = jnp.concatenate(weights, axis=1)
        innov = jnp.concatenate(innovs, axis=1)
        scaled = (pert.astype(jnp.float32) * weight).astype(jnp.bfloat16)
        precision = (members - 1) * eye + lax.dot_general(
            pert, scaled, contract_last, preferred_element_type=jnp.float32
        )
        drive = lax.dot_general(
            jnp.broadcast_to(innov, (8, innov.shape[1])).astype(jnp.bfloat16),
            scaled,
            contract_last,
            preferred_element_type=jnp.float32,
        )
        square = jnp.sum(precision * precision, axis=0, keepdims=True)
        norm = jnp.sqrt(jnp.sum(square, axis=1, keepdims=True))
        state.append((precision / norm, drive, norm))
    currents = [s[0] for s in state]
    roots = [None] * tiles
    for sweep in range(NS_ITERS):
        for t in range(tiles):
            current = split(currents[t])
            if sweep == 0:
                factor = 1.5 * eye - 0.5 * currents[t]
            else:
                factor = 1.5 * eye - 0.5 * dot3(current, split(roots[t]))
            both = split(factor)
            if sweep < NS_ITERS - 1:
                currents[t] = dot3(both, current)
            roots[t] = factor if sweep == 0 else dot3(split(roots[t]), both)
    for t in range(tiles):
        _, drive, norm = state[t]
        root = split(roots[t])
        inner = dot3(split(drive), root)
        gain = dot3(split(inner), root) / norm
        scale = jnp.sqrt((members - 1) / norm)
        final = (scale * roots[t] + gain[0:1, :]).astype(jnp.bfloat16)
        mix[t] = final
        left = 1.0 - jnp.sum(final.astype(jnp.float32), axis=1, keepdims=True)
        rest[t] = jnp.broadcast_to(left, rest.shape[1:])


def turn_in(piece, t, buf):
    rows, _, depth, points = piece.shape
    field = piece[:, t].astype(jnp.float32)
    buf[...] = field.reshape(rows * depth, points)
    turned = jnp.concatenate(
        [buf[pl.ds(level, rows, stride=depth), :] for level in range(depth)], axis=1
    )
    return turned.astype(jnp.bfloat16), jnp.sum(field, axis=0)


def gather_kernel(*refs):
    pieces, (fields, total, bufs) = refs[:-3], refs[-3:]
    rows = pieces[0].shape[0]
    for t in range(fields.shape[0]):
        acc = jnp.zeros(total.shape[1:], jnp.float32)
        for q, piece in enumerate(pieces):
            turned, part = turn_in(piece, t, bufs.at[(t * len(pieces) + q) % bufs.shape[0]])
            fields[t, q * rows:(q + 1) * rows, :] = turned
            acc += part
        total[t] = acc


def combine(t, mix, rest, field, mean, sent, first):
    depth, rows, points = sent[0][0].shape[1:]
    count = len(sent) * rows
    result = jnp.dot(
        mix[t, first:first + count, :], field, preferred_element_type=jnp.float32
    )
    for level in range(depth):
        part = result[:, level * points:(level + 1) * points]
        part = part + rest[t, first:first + count, :] * mean[level:level + 1, :]
        part = part.astype(jnp.bfloat16)
        for v, (out, start) in enumerate(sent):
            out[t - start, level] = part[v * rows:(v + 1) * rows, :]


def cut_kernel(blocks, spot, fields, *refs):
    sems = refs[-1]
    copies = []
    for q, (s, start, stop) in enumerate(blocks):
        copy = pltpu.make_async_copy(
            fields.at[:, spot[0] ^ s, pl.ds(start, stop - start)], refs[q], sems.at[q]
        )
        copy.start()
        copies.append(copy)
    for copy in copies:
        copy.wait()


def turn_late(t, pieces, starts, total, members, bufs, late_fields, mean_out, slot):
    acc = total[t]
    rows = pieces[0].shape[0]
    for q, (piece, start) in enumerate(zip(pieces, starts)):
        part, add = turn_in(piece, t - start, bufs.at[t * len(pieces) + q])
        late_fields[slot, q * rows:(q + 1) * rows, :] = part
        acc += add
    mean_out[slot] = acc / members


def lead_kernel(late, first, cut, mix, rest, fields, total, *refs):
    pieces, sent = refs[:late], refs[late:-3]
    late_fields, mean, bufs = refs[-3:]
    for t in range(cut):
        turn_late(t, pieces, [0] * late, total, mix.shape[1], bufs, late_fields, mean, t)
        field = jnp.concatenate([fields[t], late_fields[t]], axis=0)
        combine(t, mix, rest, field, mean[t], [(out, 0) for out in sent], first)


def main_kernel(late, first, lead, cut, mix, rest, fields, total, lead_fields, lead_mean, *refs):
    pieces, sent = refs[:late], refs[late:-3]
    late_fields, mean, bufs = refs[-3:]
    rows = sent[0].shape[2]
    starts = [0] * (late - 1) + [cut]
    for t in range(mix.shape[0]):
        if t < cut:
            late_fields[t] = lead_fields[t]
            mean[t] = lead_mean[t]
            outs, skip = [(out, 0) for out in sent[lead:]], lead * rows
        else:
            turn_late(t, pieces, starts, total, mix.shape[1], bufs, late_fields, mean, t)
            outs = [(out, cut if v < lead else 0) for v, out in enumerate(sent)]
            skip = 0
        field = jnp.concatenate([fields[t], late_fields[t]], axis=0)
        combine(t, mix, rest, field, mean[t], outs, first + skip)


def second_kernel(mix, rest, fields, late_fields, mean, *sent):
    for t in range(mix.shape[0]):
        field = jnp.concatenate([fields[t], late_fields[t]], axis=0)
        combine(t, mix, rest, field, mean[t], [(out, 0) for out in sent], 0)


def place_kernel(targets, aliased, spot, *refs):
    pieces = refs[:len(targets)]
    result, turned, buf, sems = refs[len(targets) + aliased:]
    copies = []
    for q, ((s, start), piece) in enumerate(zip(targets, pieces)):
        tiles, depth, rows, points = piece.shape
        for t in range(tiles):
            view = buf.at[(q * tiles + t) % buf.shape[0]]
            for level in range(depth):
                view[pl.ds(level, rows, stride=depth), :] = piece[t, level].astype(jnp.float32)
            turned[q, :, t] = view[...].reshape(rows, depth, points).astype(jnp.bfloat16)
        copy = pltpu.make_async_copy(
            turned.at[q, :, pl.ds(0, tiles)],
            result.at[:, spot[0] ^ s, pl.ds(start, tiles)],
            sems.at[q],
        )
        copy.start()
        copies.append(copy)
    for copy in copies:
        copy.wait()


def neighbours(x, axis):
    peers = lax.axis_size(axis)
    if peers == 1:
        return x, x
    if peers == 2:
        other = lax.ppermute(x, axis, [(0, 1), (1, 0)])
        return other, other
    up = [(i, i + 1) for i in range(peers - 1)]
    return lax.ppermute(x, axis, up), lax.ppermute(x, axis, [(j, i) for i, j in up])


def send_order(wide):
    far = list(range(wide // 2, wide))
    half = len(far) // 2
    return [s for pair in zip(far[half:], far[:half]) for s in pair], list(range(1, wide // 2))


def on_device(
    prior_states,
    measured_anomalies,
    departures,
    error_precisions,
    datum_totals,
    datum_patch_owner,
    patch_group_lookup,
):
    wide = lax.axis_size("wide")
    bands = lax.axis_size("band")
    me = lax.axis_index("wide").astype(jnp.int32)
    direct = wide <= DIRECT_MAX
    mine, _, _, depth, points = prior_states.shape
    blocks, members, slots = measured_anomalies.shape[1:]
    tiles, entries = patch_group_lookup.shape[1:]
    fields = prior_states.reshape(mine, wide, tiles, depth, points)
    vmem = pl.BlockSpec(memory_space=pltpu.VMEM)
    smem = pl.BlockSpec(memory_space=pltpu.SMEM)

    def call(kernel, out_shape, in_specs, scratch, limit, **more):
        out_specs = more.pop("out_specs", jax.tree.map(lambda _: vmem, out_shape))
        return pl.pallas_call(
            kernel,
            out_shape=out_shape,
            in_specs=in_specs,
            out_specs=out_specs,
            scratch_shapes=scratch,
            compiler_params=pltpu.CompilerParams(vmem_limit_bytes=limit * MIB),
            **more,
        )

    def swap(x, s):
        return lax.ppermute(x, "wide", [(i, i ^ s) for i in range(wide)])

    hbm = pl.BlockSpec(memory_space=pl.ANY)
    if direct:
        far, near_by = send_order(wide)
        late = far[-LATE:]
        early = [0] + near_by + far[:-LATE]
        order = early + late
        cut = 1 if tiles > 1 else 0

        def slices(blocks, *after):
            return call(
                functools.partial(cut_kernel, blocks),
                [
                    jax.ShapeDtypeStruct((mine, stop - start, depth, points), jnp.bfloat16)
                    for _, start, stop in blocks
                ],
                [smem, hbm],
                [pltpu.SemaphoreType.DMA((len(blocks),))],
                8,
            )(me.reshape(1), fields)

        last = far[-1]
        arrived = {}
        parts = dict(zip(far[:LEAD], slices([(s, 0, tiles) for s in far[:LEAD]])))
        others = far[LEAD:-1] + near_by + [0]
        wanted = [(s, 0, tiles) for s in others]
        wanted += [(last, 0, cut)] * (cut > 0) + [(last, cut, tiles)]
        *found, tail = slices(wanted)
        parts.update(zip(others + [last], found))
        arrived[0] = parts.pop(0)
        for s, part in parts.items():
            arrived[s] = swap(part, s)
        arrived_tail = swap(tail, last)
    else:
        order = [0]

    slot_index = jnp.arange(slots, dtype=jnp.int32)
    live = jnp.where(slot_index[None, :] < datum_totals[0][:, None], 1.0, 0.0)
    base = error_precisions[0].astype(jnp.float32) * live
    tile_ids = jnp.arange(tiles, dtype=jnp.int32)
    near = jnp.where(datum_patch_owner[0][:, None, :] == tile_ids[None, :, None], 1.0, LOC_FAR)
    pad = -(tiles + 1) % 8
    aux = jnp.concatenate(
        [
            base[:, None, :] * near,
            departures[0][:, None, :].astype(jnp.float32),
            jnp.zeros((blocks, pad, slots), jnp.float32),
        ],
        axis=1,
    )
    below, above = neighbours(measured_anomalies[0], "band")
    below_aux, above_aux = neighbours(aux, "band")
    band = lax.axis_index("band")
    below_aux = jnp.where(band > 0, below_aux, 0.0)
    above_aux = jnp.where(band < bands - 1, above_aux, 0.0)

    mix, rest = call(
        functools.partial(mix_kernel, order),
        [
            jax.ShapeDtypeStruct((tiles, members, members), jnp.bfloat16),
            jax.ShapeDtypeStruct((tiles, members, points), jnp.float32),
        ],
        [smem, smem] + [vmem] * 6,
        [pltpu.VMEM((tiles, members, entries * slots), jnp.bfloat16)],
        24,
    )(
        patch_group_lookup[0],
        me.reshape(1),
        measured_anomalies[0],
        below,
        above,
        aux,
        below_aux,
        above_aux,
    )

    if not direct:
        whole = lax.all_to_all(fields, "wide", split_axis=1, concat_axis=0, tiled=True)
        flat = whole.reshape(members, tiles, depth * points)
        mean = jnp.sum(flat, axis=0, dtype=jnp.float32) / members
        spread = (flat.astype(jnp.float32) - mean).astype(jnp.bfloat16)
        result = mean + jnp.einsum("tkj,jtp->ktp", mix, spread, preferred_element_type=jnp.float32)
        back = lax.all_to_all(
            result.astype(jnp.bfloat16).reshape(wide, mine, tiles, depth, points),
            "wide",
            split_axis=0,
            concat_axis=2,
            tiled=True,
        )
        return back.reshape(prior_states.shape)

    width = depth * points
    count = len(early) * mine
    gathered, total = call(
        gather_kernel,
        [
            jax.ShapeDtypeStruct((tiles, count, width), jnp.bfloat16),
            jax.ShapeDtypeStruct((tiles, depth, points), jnp.float32),
        ],
        [vmem] * len(early),
        [pltpu.VMEM((8, mine * depth, points), jnp.float32)],
        12,
    )(*[arrived[s] for s in early])
    close = len(near_by) + 1

    def block(count):
        return jax.ShapeDtypeStruct((count, depth, mine, points), jnp.bfloat16)

    def late_shapes(count):
        return [
            jax.ShapeDtypeStruct((count, LATE * mine, width), jnp.bfloat16),
            jax.ShapeDtypeStruct((count, depth, points), jnp.float32),
        ]

    turn_bufs = [pltpu.VMEM((tiles * LATE, mine * depth, points), jnp.float32)]
    sent, sent_lead = {}, {}
    if cut:
        *outs, lead_fields, lead_mean = call(
            functools.partial(lead_kernel, LATE, close * mine, cut),
            [block(cut)] * LEAD + late_shapes(cut),
            [vmem] * (4 + LATE),
            turn_bufs,
            12,
        )(mix, rest, gathered, total, *[arrived[s] for s in late])
        sent_lead = dict(zip(far[:LEAD], outs))
    else:
        lead_fields, lead_mean = [jnp.zeros(x.shape, x.dtype) for x in late_shapes(1)]
    *outs, late_fields, mean = call(
        functools.partial(main_kernel, LATE, close * mine, LEAD, cut),
        [block(tiles - cut)] * LEAD + [block(tiles)] * (len(far) - LEAD) + late_shapes(tiles),
        [vmem] * (6 + LATE),
        turn_bufs,
        12,
    )(
        mix, rest, gathered, total, lead_fields, lead_mean,
        *[arrived[s] for s in late[:-1]], arrived_tail,
    )
    sent = dict(zip(far, outs))
    outs = call(
        second_kernel, [block(tiles)] * close, [vmem] * 5, [], 12
    )(mix, rest, gathered, late_fields, mean)
    sent.update(zip([0] + near_by, outs))
    back = []
    for s, part in sent_lead.items():
        back.append((s, 0, swap(part, s)))
    for s in far + near_by:
        back.append((s, cut if s in sent_lead else 0, swap(sent[s], s)))
    back.append((0, 0, sent[0]))

    result = jax.ShapeDtypeStruct((mine, wide, tiles, depth, points), jnp.bfloat16)

    def place(group, *rest):
        return call(
            functools.partial(place_kernel, [(s, start) for s, start, _ in group], len(rest)),
            result,
            [smem] + [vmem] * len(group) + [hbm] * len(rest),
            [
                pltpu.VMEM((len(group), mine, tiles, depth, points), jnp.bfloat16),
                pltpu.VMEM((4, mine * depth, points), jnp.float32),
                pltpu.SemaphoreType.DMA((len(group),)),
            ],
            12,
            out_specs=hbm,
            input_output_aliases={1 + len(group): 0} if rest else {},
        )(me.reshape(1), *[part for _, _, part in group], *rest)

    most = place([x for x in back if x[0] not in late])
    final = place([x for x in back if x[0] in late], most)
    return final.reshape(prior_states.shape)


def solution(mesh):
    in_specs = (
        P("wide", "band", None, None, None),
        P("band", "wide", None, None),
        P("band", "wide", None),
        P("band", "wide", None),
        P("band", "wide"),
        P("band", "wide", None),
        P("band", "wide", None),
    )
    out_specs = P("wide", "band", None, None, None)
    return jax.shard_map(
        on_device, mesh=mesh, in_specs=in_specs, out_specs=out_specs, check_vma=False
    )
```

```python
import functools

import jax
import jax.numpy as jnp
from jax import lax
from jax.experimental import pallas as pl
from jax.experimental.pallas import tpu as pltpu
from jax.sharding import PartitionSpec as P


NS_ITERS = 6
LOC_FAR = 0.5
DIRECT_MAX = 16

LATE = 4
LEAD = 2
PLACE = (9, 14)
MIB = 1 << 20


def split(x):
    high = x.astype(jnp.bfloat16)
    return high, (x - high.astype(jnp.float32)).astype(jnp.bfloat16)


def dot3(a, b):
    (ah, al), (bh, bl) = a, b
    dot = functools.partial(jnp.dot, preferred_element_type=jnp.float32)
    return dot(ah, bh) + (dot(ah, bl) + dot(al, bh))


def mix_kernel(order, lists, spot, own, below, above, own_aux, below_aux, above_aux, mix, rest, pert_buf):
    tiles, members, _ = mix.shape
    slots = own.shape[2]
    entries = lists.shape[1]
    blocks = own.shape[0]
    rows = members // len(order)
    me = spot[0]
    contract_last = (((1,), (1,)), ((), ()))
    row = lax.broadcasted_iota(jnp.int32, (members, members), 0)
    col = lax.broadcasted_iota(jnp.int32, (members, members), 1)
    eye = jnp.where(row == col, 1.0, 0.0).astype(jnp.float32)
    state = []
    for t in range(tiles):
        weights, innovs = [], []
        for n in range(entries):
            name = lists[t, n]
            if n == 0:
                src, aux, block = below, below_aux, name
            elif n == 1:
                src, aux, block = above, above_aux, name - 2 * blocks
            else:
                src, aux, block = own, own_aux, name - blocks
            for q, u in enumerate(order):
                start = 0 if len(order) == 1 else pl.multiple_of((me ^ u) * rows, rows)
                pert_buf[t, q * rows:(q + 1) * rows, n * slots:(n + 1) * slots] = src[
                    block, pl.ds(start, rows), :
                ]
            weights.append(aux[block, t:t + 1, :])
            innovs.append(aux[block, tiles:tiles + 1, :])
        pert = pert_buf[t]
        weight = jnp.concatenate(weights, axis=1)
        innov = jnp.concatenate(innovs, axis=1)
        scaled = (pert.astype(jnp.float32) * weight).astype(jnp.bfloat16)
        precision = (members - 1) * eye + lax.dot_general(
            pert, scaled, contract_last, preferred_element_type=jnp.float32
        )
        drive = lax.dot_general(
            jnp.broadcast_to(innov, (8, innov.shape[1])).astype(jnp.bfloat16),
            scaled,
            contract_last,
            preferred_element_type=jnp.float32,
        )
        square = jnp.sum(precision * precision, axis=0, keepdims=True)
        norm = jnp.sqrt(jnp.sum(square, axis=1, keepdims=True))
        state.append((precision / norm, drive, norm))
    currents = [s[0] for s in state]
    roots = [None] * tiles
    for sweep in range(NS_ITERS):
        for t in range(tiles):
            current = split(currents[t])
            if sweep == 0:
                factor = 1.5 * eye - 0.5 * currents[t]
            else:
                factor = 1.5 * eye - 0.5 * dot3(current, split(roots[t]))
            both = split(factor)
            if sweep < NS_ITERS - 1:
                currents[t] = dot3(both, current)
            roots[t] = factor if sweep == 0 else dot3(split(roots[t]), both)
    for t in range(tiles):
        _, drive, norm = state[t]
        root = split(roots[t])
        inner = dot3(split(drive), root)
        gain = dot3(split(inner), root) / norm
        scale = jnp.sqrt((members - 1) / norm)
        final = (scale * roots[t] + gain[0:1, :]).astype(jnp.bfloat16)
        mix[t] = final
        left = 1.0 - jnp.sum(final.astype(jnp.float32), axis=1, keepdims=True)
        rest[t] = jnp.broadcast_to(left, rest.shape[1:])


def turn_in(piece, t, buf):
    rows, _, depth, points = piece.shape
    field = piece[:, t].astype(jnp.float32)
    buf[...] = field.reshape(rows * depth, points)
    turned = jnp.concatenate(
        [buf[pl.ds(level, rows, stride=depth), :] for level in range(depth)], axis=1
    )
    return turned.astype(jnp.bfloat16), jnp.sum(field, axis=0)


def gather_kernel(*refs):
    pieces, (fields, total, bufs) = refs[:-3], refs[-3:]
    rows = pieces[0].shape[0]
    for t in range(fields.shape[0]):
        acc = jnp.zeros(total.shape[1:], jnp.float32)
        for q, piece in enumerate(pieces):
            turned, part = turn_in(piece, t, bufs.at[(t * len(pieces) + q) % bufs.shape[0]])
            fields[t, q * rows:(q + 1) * rows, :] = turned
            acc += part
        total[t] = acc


def combine(t, mix, rest, field, mean, sent, first):
    depth, rows, points = sent[0][0].shape[1:]
    count = len(sent) * rows
    result = jnp.dot(
        mix[t, first:first + count, :], field, preferred_element_type=jnp.float32
    )
    for level in range(depth):
        part = result[:, level * points:(level + 1) * points]
        part = part + rest[t, first:first + count, :] * mean[level:level + 1, :]
        part = part.astype(jnp.bfloat16)
        for v, (out, start) in enumerate(sent):
            out[t - start, level] = part[v * rows:(v + 1) * rows, :]


def cut_kernel(blocks, spot, fields, *refs):
    sems = refs[-1]
    copies = []
    for q, (s, start, stop) in enumerate(blocks):
        copy = pltpu.make_async_copy(
            fields.at[:, spot[0] ^ s, pl.ds(start, stop - start)], refs[q], sems.at[q]
        )
        copy.start()
        copies.append(copy)
    for copy in copies:
        copy.wait()


def turn_late(t, pieces, starts, total, members, bufs, late_fields, mean_out, slot):
    acc = total[t]
    rows = pieces[0].shape[0]
    for q, (piece, start) in enumerate(zip(pieces, starts)):
        part, add = turn_in(piece, t - start, bufs.at[t * len(pieces) + q])
        late_fields[slot, q * rows:(q + 1) * rows, :] = part
        acc += add
    mean_out[slot] = acc / members


def lead_kernel(late, first, cut, mix, rest, fields, total, *refs):
    pieces, sent = refs[:late], refs[late:-3]
    late_fields, mean, bufs = refs[-3:]
    for t in range(cut):
        turn_late(t, pieces, [0] * late, total, mix.shape[1], bufs, late_fields, mean, t)
        field = jnp.concatenate([fields[t], late_fields[t]], axis=0)
        combine(t, mix, rest, field, mean[t], [(out, 0) for out in sent], first)


def main_kernel(late, first, lead, cut, mix, rest, fields, total, lead_fields, lead_mean, *refs):
    pieces, sent = refs[:late], refs[late:-3]
    late_fields, mean, bufs = refs[-3:]
    rows = sent[0].shape[2]
    starts = [0] * (late - 1) + [cut]
    for t in range(mix.shape[0]):
        if t < cut:
            late_fields[t] = lead_fields[t]
            mean[t] = lead_mean[t]
            outs, skip = [(out, 0) for out in sent[lead:]], lead * rows
        else:
            turn_late(t, pieces, starts, total, mix.shape[1], bufs, late_fields, mean, t)
            outs = [(out, cut if v < lead else 0) for v, out in enumerate(sent)]
            skip = 0
        field = jnp.concatenate([fields[t], late_fields[t]], axis=0)
        combine(t, mix, rest, field, mean[t], outs, first + skip)


def second_kernel(mix, rest, fields, late_fields, mean, *sent):
    for t in range(mix.shape[0]):
        field = jnp.concatenate([fields[t], late_fields[t]], axis=0)
        combine(t, mix, rest, field, mean[t], [(out, 0) for out in sent], 0)


def place_kernel(targets, aliased, spot, *refs):
    pieces = refs[:len(targets)]
    result, turned, buf, sems = refs[len(targets) + aliased:]
    copies = []
    for q, ((s, start), piece) in enumerate(zip(targets, pieces)):
        tiles, depth, rows, points = piece.shape
        for t in range(tiles):
            view = buf.at[(q * tiles + t) % buf.shape[0]]
            for level in range(depth):
                view[pl.ds(level, rows, stride=depth), :] = piece[t, level].astype(jnp.float32)
            turned[q, :, t] = view[...].reshape(rows, depth, points).astype(jnp.bfloat16)
        copy = pltpu.make_async_copy(
            turned.at[q, :, pl.ds(0, tiles)],
            result.at[:, spot[0] ^ s, pl.ds(start, tiles)],
            sems.at[q],
        )
        copy.start()
        copies.append(copy)
    for copy in copies:
        copy.wait()


def neighbours(x, axis):
    peers = lax.axis_size(axis)
    if peers == 1:
        return x, x
    if peers == 2:
        other = lax.ppermute(x, axis, [(0, 1), (1, 0)])
        return other, other
    up = [(i, i + 1) for i in range(peers - 1)]
    return lax.ppermute(x, axis, up), lax.ppermute(x, axis, [(j, i) for i, j in up])


def send_order(wide):
    near = list(range(1, wide // 2))
    return list(range(wide // 2, wide)), near[wide // 4 - 1:] + near[:wide // 4 - 1]


def interleave(a, b):
    mixed = []
    for k, s in enumerate(a):
        mixed += [s] + b[k:k + 1]
    return mixed + b[len(a):]


def on_device(
    prior_states,
    measured_anomalies,
    departures,
    error_precisions,
    datum_totals,
    datum_patch_owner,
    patch_group_lookup,
):
    wide = lax.axis_size("wide")
    bands = lax.axis_size("band")
    me = lax.axis_index("wide").astype(jnp.int32)
    direct = wide <= DIRECT_MAX
    mine, _, _, depth, points = prior_states.shape
    blocks, members, slots = measured_anomalies.shape[1:]
    tiles, entries = patch_group_lookup.shape[1:]
    fields = prior_states.reshape(mine, wide, tiles, depth, points)
    vmem = pl.BlockSpec(memory_space=pltpu.VMEM)
    smem = pl.BlockSpec(memory_space=pltpu.SMEM)

    def call(kernel, out_shape, in_specs, scratch, limit, **more):
        out_specs = more.pop("out_specs", jax.tree.map(lambda _: vmem, out_shape))
        return pl.pallas_call(
            kernel,
            out_shape=out_shape,
            in_specs=in_specs,
            out_specs=out_specs,
            scratch_shapes=scratch,
            compiler_params=pltpu.CompilerParams(vmem_limit_bytes=limit * MIB),
            **more,
        )

    def swap(x, s):
        return lax.ppermute(x, "wide", [(i, i ^ s) for i in range(wide)])

    hbm = pl.BlockSpec(memory_space=pl.ANY)
    if direct:
        far, near_by = send_order(wide)
        late = far[-LATE:]
        early = [0] + near_by + far[:-LATE]
        order = early + late
        cut = 1 if tiles > 1 else 0

        def slices(blocks, *after):
            return call(
                functools.partial(cut_kernel, blocks),
                [
                    jax.ShapeDtypeStruct((mine, stop - start, depth, points), jnp.bfloat16)
                    for _, start, stop in blocks
                ],
                [smem, pl.BlockSpec(memory_space=pltpu.HBM)],
                [pltpu.SemaphoreType.DMA((len(blocks),))],
                8,
            )(me.reshape(1), fields)

        last = far[-1]
        arrived = {}
        parts = dict(zip(far[:LEAD], slices([(s, 0, tiles) for s in far[:LEAD]])))
        others = far[LEAD:-1] + near_by + [0]
        wanted = [(s, 0, tiles) for s in others]
        wanted += [(last, 0, cut)] * (cut > 0) + [(last, cut, tiles)]
        *found, tail = slices(wanted)
        parts.update(zip(others + [last], found))
        arrived[0] = parts.pop(0)
        for s, part in parts.items():
            arrived[s] = swap(part, s)
        arrived_tail = swap(tail, last)
    else:
        order = [0]

    slot_index = jnp.arange(slots, dtype=jnp.int32)
    live = jnp.where(slot_index[None, :] < datum_totals[0][:, None], 1.0, 0.0)
    base = error_precisions[0].astype(jnp.float32) * live
    tile_ids = jnp.arange(tiles, dtype=jnp.int32)
    near = jnp.where(datum_patch_owner[0][:, None, :] == tile_ids[None, :, None], 1.0, LOC_FAR)
    pad = -(tiles + 1) % 8
    aux = jnp.concatenate(
        [
            base[:, None, :] * near,
            departures[0][:, None, :].astype(jnp.float32),
            jnp.zeros((blocks, pad, slots), jnp.float32),
        ],
        axis=1,
    )
    below, above = neighbours(measured_anomalies[0], "band")
    below_aux, above_aux = neighbours(aux, "band")
    band = lax.axis_index("band")
    below_aux = jnp.where(band > 0, below_aux, 0.0)
    above_aux = jnp.where(band < bands - 1, above_aux, 0.0)

    mix, rest = call(
        functools.partial(mix_kernel, order),
        [
            jax.ShapeDtypeStruct((tiles, members, members), jnp.bfloat16),
            jax.ShapeDtypeStruct((tiles, members, points), jnp.float32),
        ],
        [smem, smem] + [vmem] * 6,
        [pltpu.VMEM((tiles, members, entries * slots), jnp.bfloat16)],
        24,
    )(
        patch_group_lookup[0],
        me.reshape(1),
        measured_anomalies[0],
        below,
        above,
        aux,
        below_aux,
        above_aux,
    )

    if not direct:
        whole = lax.all_to_all(fields, "wide", split_axis=1, concat_axis=0, tiled=True)
        flat = whole.reshape(members, tiles, depth * points)
        mean = jnp.sum(flat, axis=0, dtype=jnp.float32) / members
        spread = (flat.astype(jnp.float32) - mean).astype(jnp.bfloat16)
        result = mean + jnp.einsum("tkj,jtp->ktp", mix, spread, preferred_element_type=jnp.float32)
        back = lax.all_to_all(
            result.astype(jnp.bfloat16).reshape(wide, mine, tiles, depth, points),
            "wide",
            split_axis=0,
            concat_axis=2,
            tiled=True,
        )
        return back.reshape(prior_states.shape)

    width = depth * points
    count = len(early) * mine
    gathered, total = call(
        gather_kernel,
        [
            jax.ShapeDtypeStruct((tiles, count, width), jnp.bfloat16),
            jax.ShapeDtypeStruct((tiles, depth, points), jnp.float32),
        ],
        [vmem] * len(early),
        [pltpu.VMEM((8, mine * depth, points), jnp.float32)],
        12,
    )(*[arrived[s] for s in early])
    close = len(near_by) + 1

    def block(count):
        return jax.ShapeDtypeStruct((count, depth, mine, points), jnp.bfloat16)

    def late_shapes(count):
        return [
            jax.ShapeDtypeStruct((count, LATE * mine, width), jnp.bfloat16),
            jax.ShapeDtypeStruct((count, depth, points), jnp.float32),
        ]

    turn_bufs = [pltpu.VMEM((tiles * LATE, mine * depth, points), jnp.float32)]
    sent, sent_lead = {}, {}
    if cut:
        *outs, lead_fields, lead_mean = call(
            functools.partial(lead_kernel, LATE, close * mine, cut),
            [block(cut)] * LEAD + late_shapes(cut),
            [vmem] * (4 + LATE),
            turn_bufs,
            12,
        )(mix, rest, gathered, total, *[arrived[s] for s in late])
        sent_lead = dict(zip(far[:LEAD], outs))
    else:
        lead_fields, lead_mean = [jnp.zeros(x.shape, x.dtype) for x in late_shapes(1)]
    *outs, late_fields, mean = call(
        functools.partial(main_kernel, LATE, close * mine, LEAD, cut),
        [block(tiles - cut)] * LEAD + [block(tiles)] * (len(far) - LEAD) + late_shapes(tiles),
        [vmem] * (6 + LATE),
        turn_bufs,
        12,
    )(
        mix, rest, gathered, total, lead_fields, lead_mean,
        *[arrived[s] for s in late[:-1]], arrived_tail,
    )
    sent = dict(zip(far, outs))
    outs = call(
        second_kernel, [block(tiles)] * close, [vmem] * 5, [], 12
    )(mix, rest, gathered, late_fields, mean)
    sent.update(zip([0] + near_by, outs))
    back = []
    for s, part in sent_lead.items():
        back.append((s, 0, swap(part, s)))
    for s in far + near_by:
        back.append((s, cut if s in sent_lead else 0, swap(sent[s], s)))
    back.append((0, 0, sent[0]))

    result = jax.ShapeDtypeStruct((mine, wide, tiles, depth, points), jnp.bfloat16)

    def place(group, *rest):
        return call(
            functools.partial(place_kernel, [(s, start) for s, start, _ in group], len(rest)),
            result,
            [smem] + [vmem] * len(group) + [hbm] * len(rest),
            [
                pltpu.VMEM((len(group), mine, tiles, depth, points), jnp.bfloat16),
                pltpu.VMEM((4, mine * depth, points), jnp.float32),
                pltpu.SemaphoreType.DMA((len(group),)),
            ],
            12,
            out_specs=hbm,
            input_output_aliases={1 + len(group): 0} if rest else {},
        )(me.reshape(1), *[part for _, _, part in group], *rest)

    turn = {s: k for k, s in enumerate([0] + far[:LEAD] + interleave(far[LEAD:], near_by))}
    back.sort(key=lambda x: turn[x[0]])
    final = []
    for start, stop in zip((0,) + PLACE, PLACE + (len(back),)):
        final = [place(back[start:stop], *final)]
    return final[0].reshape(prior_states.shape)


def solution(mesh):
    in_specs = (
        P("wide", "band", None, None, None),
        P("band", "wide", None, None),
        P("band", "wide", None),
        P("band", "wide", None),
        P("band", "wide"),
        P("band", "wide", None),
        P("band", "wide", None),
    )
    out_specs = P("wide", "band", None, None, None)
    return jax.shard_map(
        on_device, mesh=mesh, in_specs=in_specs, out_specs=out_specs, check_vma=False
    )
```

```python
import functools

import jax
import jax.numpy as jnp
from jax import lax
from jax.experimental import pallas as pl
from jax.experimental.pallas import tpu as pltpu
from jax.sharding import PartitionSpec as P


NS_ITERS = 6
LOC_FAR = 0.5
DIRECT_MAX = 16

LATE = 4
LEAD = 2
PLACE = (9, 14)
MIB = 1 << 20


def split(x):
    high = x.astype(jnp.bfloat16)
    return high, (x - high.astype(jnp.float32)).astype(jnp.bfloat16)


def dot3(a, b):
    (ah, al), (bh, bl) = a, b
    dot = functools.partial(jnp.dot, preferred_element_type=jnp.float32)
    return dot(ah, bh) + (dot(ah, bl) + dot(al, bh))


def mix_kernel(order, lists, spot, own, below, above, own_aux, below_aux, above_aux, mix, rest, pert_buf):
    tiles, members, _ = mix.shape
    slots = own.shape[2]
    entries = lists.shape[1]
    blocks = own.shape[0]
    rows = members // len(order)
    me = spot[0]
    contract_last = (((1,), (1,)), ((), ()))
    row = lax.broadcasted_iota(jnp.int32, (members, members), 0)
    col = lax.broadcasted_iota(jnp.int32, (members, members), 1)
    eye = jnp.where(row == col, 1.0, 0.0).astype(jnp.float32)
    state = []
    for t in range(tiles):
        weights, innovs = [], []
        for n in range(entries):
            name = lists[t, n]
            if n == 0:
                src, aux, block = below, below_aux, name
            elif n == 1:
                src, aux, block = above, above_aux, name - 2 * blocks
            else:
                src, aux, block = own, own_aux, name - blocks
            for q, u in enumerate(order):
                start = 0 if len(order) == 1 else pl.multiple_of((me ^ u) * rows, rows)
                pert_buf[t, q * rows:(q + 1) * rows, n * slots:(n + 1) * slots] = src[
                    block, pl.ds(start, rows), :
                ]
            weights.append(aux[block, t:t + 1, :])
            innovs.append(aux[block, tiles:tiles + 1, :])
        pert = pert_buf[t]
        weight = jnp.concatenate(weights, axis=1)
        innov = jnp.concatenate(innovs, axis=1)
        scaled = (pert.astype(jnp.float32) * weight).astype(jnp.bfloat16)
        precision = (members - 1) * eye + lax.dot_general(
            pert, scaled, contract_last, preferred_element_type=jnp.float32
        )
        drive = lax.dot_general(
            jnp.broadcast_to(innov, (8, innov.shape[1])).astype(jnp.bfloat16),
            scaled,
            contract_last,
            preferred_element_type=jnp.float32,
        )
        square = jnp.sum(precision * precision, axis=0, keepdims=True)
        norm = jnp.sqrt(jnp.sum(square, axis=1, keepdims=True))
        state.append((precision / norm, drive, norm))
    currents = [s[0] for s in state]
    roots = [None] * tiles
    for sweep in range(NS_ITERS):
        for t in range(tiles):
            current = split(currents[t])
            if sweep == 0:
                factor = 1.5 * eye - 0.5 * currents[t]
            else:
                factor = 1.5 * eye - 0.5 * dot3(current, split(roots[t]))
            both = split(factor)
            if sweep < NS_ITERS - 1:
                currents[t] = dot3(both, current)
            roots[t] = factor if sweep == 0 else dot3(split(roots[t]), both)
    for t in range(tiles):
        _, drive, norm = state[t]
        root = split(roots[t])
        inner = dot3(split(drive), root)
        gain = dot3(split(inner), root) / norm
        scale = jnp.sqrt((members - 1) / norm)
        final = (scale * roots[t] + gain[0:1, :]).astype(jnp.bfloat16)
        mix[t] = final
        left = 1.0 - jnp.sum(final.astype(jnp.float32), axis=1, keepdims=True)
        rest[t] = jnp.broadcast_to(left, rest.shape[1:])


def turn_in(piece, t, buf):
    rows, _, depth, points = piece.shape
    field = piece[:, t].astype(jnp.float32)
    buf[...] = field.reshape(rows * depth, points)
    turned = jnp.concatenate(
        [buf[pl.ds(level, rows, stride=depth), :] for level in range(depth)], axis=1
    )
    return turned.astype(jnp.bfloat16), jnp.sum(field, axis=0)


def gather_kernel(*refs):
    pieces, (fields, total, bufs) = refs[:-3], refs[-3:]
    rows = pieces[0].shape[0]
    for t in range(fields.shape[0]):
        acc = jnp.zeros(total.shape[1:], jnp.float32)
        for q, piece in enumerate(pieces):
            turned, part = turn_in(piece, t, bufs.at[(t * len(pieces) + q) % bufs.shape[0]])
            fields[t, q * rows:(q + 1) * rows, :] = turned
            acc += part
        total[t] = acc


def combine(t, mix, rest, field, mean, sent, first):
    depth, rows, points = sent[0][0].shape[1:]
    count = len(sent) * rows
    result = jnp.dot(
        mix[t, first:first + count, :], field, preferred_element_type=jnp.float32
    )
    for level in range(depth):
        part = result[:, level * points:(level + 1) * points]
        part = part + rest[t, first:first + count, :] * mean[level:level + 1, :]
        part = part.astype(jnp.bfloat16)
        for v, (out, start) in enumerate(sent):
            out[t - start, level] = part[v * rows:(v + 1) * rows, :]


def cut_kernel(blocks, spot, fields, *refs):
    sems = refs[-1]
    copies = []
    for q, (s, start, stop) in enumerate(blocks):
        copy = pltpu.make_async_copy(
            fields.at[:, spot[0] ^ s, pl.ds(start, stop - start)], refs[q], sems.at[q]
        )
        copy.start()
        copies.append(copy)
    for copy in copies:
        copy.wait()


def turn_late(t, pieces, starts, total, members, bufs, late_fields, mean_out, slot):
    acc = total[t]
    rows = pieces[0].shape[0]
    for q, (piece, start) in enumerate(zip(pieces, starts)):
        part, add = turn_in(piece, t - start, bufs.at[t * len(pieces) + q])
        late_fields[slot, q * rows:(q + 1) * rows, :] = part
        acc += add
    mean_out[slot] = acc / members


def lead_kernel(late, first, cut, mix, rest, fields, total, *refs):
    pieces, sent = refs[:late], refs[late:-3]
    late_fields, mean, bufs = refs[-3:]
    for t in range(cut):
        turn_late(t, pieces, [0] * late, total, mix.shape[1], bufs, late_fields, mean, t)
        field = jnp.concatenate([fields[t], late_fields[t]], axis=0)
        combine(t, mix, rest, field, mean[t], [(out, 0) for out in sent], first)


def main_kernel(late, first, lead, cut, mix, rest, fields, total, lead_fields, lead_mean, *refs):
    pieces, sent = refs[:late], refs[late:-3]
    late_fields, mean, bufs = refs[-3:]
    rows = sent[0].shape[2]
    starts = [0] * (late - 1) + [cut]
    for t in range(mix.shape[0]):
        if t < cut:
            late_fields[t] = lead_fields[t]
            mean[t] = lead_mean[t]
            outs, skip = [(out, 0) for out in sent[lead:]], lead * rows
        else:
            turn_late(t, pieces, starts, total, mix.shape[1], bufs, late_fields, mean, t)
            outs = [(out, cut if v < lead else 0) for v, out in enumerate(sent)]
            skip = 0
        field = jnp.concatenate([fields[t], late_fields[t]], axis=0)
        combine(t, mix, rest, field, mean[t], outs, first + skip)


def second_kernel(mix, rest, fields, late_fields, mean, *sent):
    for t in range(mix.shape[0]):
        field = jnp.concatenate([fields[t], late_fields[t]], axis=0)
        combine(t, mix, rest, field, mean[t], [(out, 0) for out in sent], 0)


def place_kernel(targets, aliased, spot, *refs):
    pieces = refs[:len(targets)]
    result, turned, buf, sems = refs[len(targets) + aliased:]
    copies = []
    for q, ((s, start), piece) in enumerate(zip(targets, pieces)):
        tiles, depth, rows, points = piece.shape
        for t in range(tiles):
            view = buf.at[(q * tiles + t) % buf.shape[0]]
            for level in range(depth):
                view[pl.ds(level, rows, stride=depth), :] = piece[t, level].astype(jnp.float32)
            turned[q, :, t] = view[...].reshape(rows, depth, points).astype(jnp.bfloat16)
        copy = pltpu.make_async_copy(
            turned.at[q, :, pl.ds(0, tiles)],
            result.at[:, spot[0] ^ s, pl.ds(start, tiles)],
            sems.at[q],
        )
        copy.start()
        copies.append(copy)
    for copy in copies:
        copy.wait()


def neighbours(x, axis):
    peers = lax.axis_size(axis)
    if peers == 1:
        return x, x
    if peers == 2:
        other = lax.ppermute(x, axis, [(0, 1), (1, 0)])
        return other, other
    up = [(i, i + 1) for i in range(peers - 1)]
    return lax.ppermute(x, axis, up), lax.ppermute(x, axis, [(j, i) for i, j in up])


def send_order(wide):
    near = list(range(1, wide // 2))
    return list(range(wide // 2, wide)), near[wide // 4 - 1:] + near[:wide // 4 - 1]


def interleave(a, b):
    mixed = []
    for k, s in enumerate(a):
        mixed += [s] + b[k:k + 1]
    return mixed + b[len(a):]


def on_device(
    prior_states,
    measured_anomalies,
    departures,
    error_precisions,
    datum_totals,
    datum_patch_owner,
    patch_group_lookup,
):
    wide = lax.axis_size("wide")
    bands = lax.axis_size("band")
    me = lax.axis_index("wide").astype(jnp.int32)
    direct = wide <= DIRECT_MAX
    mine, _, _, depth, points = prior_states.shape
    blocks, members, slots = measured_anomalies.shape[1:]
    tiles, entries = patch_group_lookup.shape[1:]
    fields = prior_states.reshape(mine, wide, tiles, depth, points)
    vmem = pl.BlockSpec(memory_space=pltpu.VMEM)
    smem = pl.BlockSpec(memory_space=pltpu.SMEM)

    def call(kernel, out_shape, in_specs, scratch, limit, **more):
        out_specs = more.pop("out_specs", jax.tree.map(lambda _: vmem, out_shape))
        return pl.pallas_call(
            kernel,
            out_shape=out_shape,
            in_specs=in_specs,
            out_specs=out_specs,
            scratch_shapes=scratch,
            compiler_params=pltpu.CompilerParams(vmem_limit_bytes=limit * MIB),
            **more,
        )

    def swap(x, s):
        return lax.ppermute(x, "wide", [(i, i ^ s) for i in range(wide)])

    hbm = pl.BlockSpec(memory_space=pl.ANY)
    if direct:
        far, near_by = send_order(wide)
        late = far[-LATE:]
        early = [0] + near_by + far[:-LATE]
        order = early + late
        cut = tiles // 2

        def slices(blocks, *after):
            return call(
                functools.partial(cut_kernel, blocks),
                [
                    pltpu.VMEM((mine, stop - start, depth, points), jnp.bfloat16)
                    for _, start, stop in blocks
                ],
                [smem, pl.BlockSpec(memory_space=pltpu.HBM)],
                [pltpu.SemaphoreType.DMA((len(blocks),))],
                8,
            )(me.reshape(1), fields)

        last = far[-1]
        arrived = {}
        parts = {far[0]: lax.dynamic_index_in_dim(fields, me ^ far[0], 1, keepdims=False)}
        others = far[1:-1] + near_by + [0]
        wanted = [(s, 0, tiles) for s in others]
        wanted += [(last, 0, cut)] * (cut > 0) + [(last, cut, tiles)]
        *found, tail = slices(wanted)
        parts.update(zip(others + [last], found))
        arrived[0] = parts.pop(0)
        for s, part in parts.items():
            arrived[s] = swap(part, s)
        arrived_tail = swap(tail, last)
    else:
        order = [0]

    slot_index = jnp.arange(slots, dtype=jnp.int32)
    live = jnp.where(slot_index[None, :] < datum_totals[0][:, None], 1.0, 0.0)
    base = error_precisions[0].astype(jnp.float32) * live
    tile_ids = jnp.arange(tiles, dtype=jnp.int32)
    near = jnp.where(datum_patch_owner[0][:, None, :] == tile_ids[None, :, None], 1.0, LOC_FAR)
    pad = -(tiles + 1) % 8
    aux = jnp.concatenate(
        [
            base[:, None, :] * near,
            departures[0][:, None, :].astype(jnp.float32),
            jnp.zeros((blocks, pad, slots), jnp.float32),
        ],
        axis=1,
    )
    below, above = neighbours(measured_anomalies[0], "band")
    below_aux, above_aux = neighbours(aux, "band")
    band = lax.axis_index("band")
    below_aux = jnp.where(band > 0, below_aux, 0.0)
    above_aux = jnp.where(band < bands - 1, above_aux, 0.0)

    mix, rest = call(
        functools.partial(mix_kernel, order),
        [
            jax.ShapeDtypeStruct((tiles, members, members), jnp.bfloat16),
            jax.ShapeDtypeStruct((tiles, members, points), jnp.float32),
        ],
        [smem, smem] + [vmem] * 6,
        [pltpu.VMEM((tiles, members, entries * slots), jnp.bfloat16)],
        24,
    )(
        patch_group_lookup[0],
        me.reshape(1),
        measured_anomalies[0],
        below,
        above,
        aux,
        below_aux,
        above_aux,
    )

    if not direct:
        whole = lax.all_to_all(fields, "wide", split_axis=1, concat_axis=0, tiled=True)
        flat = whole.reshape(members, tiles, depth * points)
        mean = jnp.sum(flat, axis=0, dtype=jnp.float32) / members
        spread = (flat.astype(jnp.float32) - mean).astype(jnp.bfloat16)
        result = mean + jnp.einsum("tkj,jtp->ktp", mix, spread, preferred_element_type=jnp.float32)
        back = lax.all_to_all(
            result.astype(jnp.bfloat16).reshape(wide, mine, tiles, depth, points),
            "wide",
            split_axis=0,
            concat_axis=2,
            tiled=True,
        )
        return back.reshape(prior_states.shape)

    width = depth * points
    count = len(early) * mine
    gathered, total = call(
        gather_kernel,
        [
            jax.ShapeDtypeStruct((tiles, count, width), jnp.bfloat16),
            jax.ShapeDtypeStruct((tiles, depth, points), jnp.float32),
        ],
        [vmem] * len(early),
        [pltpu.VMEM((8, mine * depth, points), jnp.float32)],
        12,
    )(*[arrived[s] for s in early])
    close = len(near_by) + 1

    def block(count):
        return jax.ShapeDtypeStruct((count, depth, mine, points), jnp.bfloat16)

    def late_shapes(count):
        return [
            jax.ShapeDtypeStruct((count, LATE * mine, width), jnp.bfloat16),
            jax.ShapeDtypeStruct((count, depth, points), jnp.float32),
        ]

    turn_bufs = [pltpu.VMEM((tiles * LATE, mine * depth, points), jnp.float32)]
    sent, sent_lead = {}, {}
    if cut:
        *outs, lead_fields, lead_mean = call(
            functools.partial(lead_kernel, LATE, close * mine, cut),
            [block(cut)] * LEAD + late_shapes(cut),
            [vmem] * (4 + LATE),
            turn_bufs,
            12,
        )(mix, rest, gathered, total, *[arrived[s] for s in late])
        sent_lead = dict(zip(far[:LEAD], outs))
    else:
        lead_fields, lead_mean = [jnp.zeros(x.shape, x.dtype) for x in late_shapes(1)]
    *outs, late_fields, mean = call(
        functools.partial(main_kernel, LATE, close * mine, LEAD, cut),
        [block(tiles - cut)] * LEAD + [block(tiles)] * (len(far) - LEAD) + late_shapes(tiles),
        [vmem] * (6 + LATE),
        turn_bufs,
        12,
    )(
        mix, rest, gathered, total, lead_fields, lead_mean,
        *[arrived[s] for s in late[:-1]], arrived_tail,
    )
    sent = dict(zip(far, outs))
    outs = call(
        second_kernel, [block(tiles)] * close, [vmem] * 5, [], 12
    )(mix, rest, gathered, late_fields, mean)
    sent.update(zip([0] + near_by, outs))
    back = []
    for s, part in sent_lead.items():
        back.append((s, 0, swap(part, s)))
    for s in far + near_by:
        back.append((s, cut if s in sent_lead else 0, swap(sent[s], s)))
    back.append((0, 0, sent[0]))

    result = jax.ShapeDtypeStruct((mine, wide, tiles, depth, points), jnp.bfloat16)

    def place(group, *rest):
        return call(
            functools.partial(place_kernel, [(s, start) for s, start, _ in group], len(rest)),
            result,
            [smem] + [vmem] * len(group) + [hbm] * len(rest),
            [
                pltpu.VMEM((len(group), mine, tiles, depth, points), jnp.bfloat16),
                pltpu.VMEM((4, mine * depth, points), jnp.float32),
                pltpu.SemaphoreType.DMA((len(group),)),
            ],
            12,
            out_specs=hbm,
            input_output_aliases={1 + len(group): 0} if rest else {},
        )(me.reshape(1), *[part for _, _, part in group], *rest)

    turn = {s: k for k, s in enumerate([0] + far[:LEAD] + interleave(far[LEAD:], near_by))}
    back.sort(key=lambda x: turn[x[0]])
    final = []
    for start, stop in zip((0,) + PLACE, PLACE + (len(back),)):
        final = [place(back[start:stop], *final)]
    return final[0].reshape(prior_states.shape)


def solution(mesh):
    in_specs = (
        P("wide", "band", None, None, None),
        P("band", "wide", None, None),
        P("band", "wide", None),
        P("band", "wide", None),
        P("band", "wide"),
        P("band", "wide", None),
        P("band", "wide", None),
    )
    out_specs = P("wide", "band", None, None, None)
    return jax.shard_map(
        on_device, mesh=mesh, in_specs=in_specs, out_specs=out_specs, check_vma=False
    )
```
